32 devices in a mesh: row: 4 (over z), col: 8 (over y, x, core).
Axes of the slice: x: 2, y: 2, z: 4, core: 2. Of those that a mesh axis runs over, the one named last changes fastest.
Arguments:
- occupations: int32 [4096, 128], P('row'), may hold values from 0 to 2
- table: float32 [384, 1024], replicated, may hold values from -0.5 to 0.5
- weights: float32 [2, 1024, 4096], P(None, None, 'col'), may hold values from -0.1875 to 0.1875
- biases: float32 [2, 4096], P(None, 'col'), may hold values from -6 to 6
- heads: float32 [2, 4096], P(None, 'col'), may hold values from -18 to 18
- energies: float32 [4096], P('row'), may hold values from -6 to 6
Outputs:
- schur: float32 [4096, 4096], P('row', 'col')
- solved_rhs: float32 [4096], P('row')
The draws below stay inside these ranges and needn't reach their ends.
All inputs are finite; a program needn't handle non-finite values.
Results may differ from the reference program's by a relative error of at most 0.0034.
Values may be sent and summed in bfloat16 or wider, within the bound.
A program may use at most 128 MiB of HBM per device.

```python
import math
import jax
import jax.numpy as jnp
from jax import lax

D = 1024
FF = 4096
ORB = 128
NSAMP = 4096
PANEL = 512


def draw_occupations(key, part):
    uniform_ints = jax.random.randint(jax.random.fold_in(key, 11), (NSAMP, ORB), 0, 1000)
    orbital_shift = jax.random.randint(jax.random.fold_in(key, 12), (ORB,), 0, 200)
    sample_ids = jnp.arange(NSAMP, dtype=jnp.int32)[:, None]
    threshold = 100 + 600 * sample_ids // NSAMP + orbital_shift[None, :]
    single = (uniform_ints < threshold).astype(jnp.int32)
    double = (uniform_ints < threshold // 3).astype(jnp.int32)
    return single + double


def block_levels(rng, shape, pieces, smallest, largest):
    def one(position, shards_of):
        heights = jax.random.uniform(jax.random.fold_in(jax.random.fold_in(rng, 6), position), (shards_of,), jnp.float32, smallest / len(pieces), largest / len(pieces))
        return jnp.repeat(jnp.exp(heights), shape[position] // shards_of).reshape((-1,) + (1,) * (len(shape) - position - 1))

    loudness = one(*pieces[0])
    for cut in pieces[1:]:
        loudness = loudness * one(*cut)
    return loudness


def centred(stream_key, dims, width, reach, split=(), held_as=jnp.bfloat16):
    level = block_levels(stream_key, dims, split, -0.22, 0.18) if split else 1.0
    entries = jax.random.normal(stream_key, dims, jnp.float32) * width * level
    return jnp.minimum(jnp.maximum(entries, -reach), reach).astype(held_as)


def setup_inputs(seed: int = 0) -> dict:
    seeds = jax.random.split(jax.random.key(seed), 7)
    return {
        "occupations": draw_occupations(jax.random.fold_in(seeds[6], 71), 0),
        "table": centred(seeds[1], (3 * ORB, D), ORB ** -0.5, 0.5, (), jnp.float32),
        "weights": centred(seeds[2], (2, D, FF), D ** -0.5, 0.1875, ((2, 8),), jnp.float32),
        "biases": centred(seeds[3], (2, FF), 1.0, 6.0, ((1, 8),), jnp.float32),
        "heads": centred(seeds[4], (2, FF), 3.0, 18.0, ((1, 8),), jnp.float32),
        "energies": centred(seeds[5], (NSAMP,), 1.0, 6.0, ((0, 4),), jnp.float32),
    }


norm_eps = 1e-06
diag_shift = 0.05

def jacobian(occupations, table, weights, biases, heads):
    onehot = jnp.concatenate([(occupations == 0).astype(jnp.float32), (occupations == 1).astype(jnp.float32), (occupations == 2).astype(jnp.float32)], axis=1)
    embedded = jnp.dot(onehot.astype(jnp.float32), table.astype(jnp.float32), precision=lax.Precision.HIGHEST, preferred_element_type=jnp.float32)
    embedded = embedded * lax.rsqrt(lax.optimization_barrier(jnp.mean(embedded * embedded, axis=-1, keepdims=True)) + norm_eps)
    blocks = []
    for panel_index in range(2):
        hidden = jnp.dot(embedded.astype(jnp.float32), weights[panel_index].astype(jnp.float32), precision=lax.Precision.HIGHEST, preferred_element_type=jnp.float32) + biases[panel_index]
        blocks.append(heads[panel_index] * jax.nn.sigmoid(hidden))
    return jnp.concatenate(blocks, axis=1)

def reference(occupations, table, weights, biases, heads, energies):
    derivs = jacobian(occupations, table, weights, biases, heads)
    sample_total = derivs.shape[0]
    centered = ((derivs - lax.optimization_barrier(jnp.sum(derivs, axis=0)) / sample_total) * (1.0 / math.sqrt(sample_total))).astype(jnp.bfloat16)
    kernel = jnp.dot(centered.astype(jnp.float32), centered.T.astype(jnp.float32), preferred_element_type=jnp.float32)
    kernel = kernel + diag_shift * jnp.eye(sample_total, dtype=jnp.float32)
    right_side = energies
    for panel_index in range(2):
        start = panel_index * PANEL
        diag_block = kernel[start:start + PANEL, start:start + PANEL]
        factor = jnp.linalg.cholesky(diag_block)
        column = kernel[:, start:start + PANEL]
        left_rows = lax.linalg.triangular_solve(factor, column, left_side=False, lower=True, transpose_a=True)
        kernel = kernel - jnp.dot(left_rows.astype(jnp.float32), left_rows.T.astype(jnp.float32), precision=lax.Precision.HIGHEST, preferred_element_type=jnp.float32)
        solved = lax.linalg.triangular_solve(factor, right_side[start:start + PANEL][:, None], left_side=True, lower=True)[:, 0]
        right_side = right_side - jnp.dot(left_rows.astype(jnp.float32), solved.astype(jnp.float32), precision=lax.Precision.HIGHEST, preferred_element_type=jnp.float32)
        right_side = right_side.at[start:start + PANEL].set(solved)
    return (kernel, right_side)
```

```python
import functools
import math

import jax
import jax.numpy as jnp
from jax import lax
from jax.experimental import pallas as pl
from jax.experimental.pallas import tpu as pltpu
from jax.sharding import PartitionSpec as P

norm_eps = 1e-06
diag_shift = 0.05
BLOCK = 128
BF = jnp.bfloat16
F32 = jnp.float32


def split3(x):
    terms = []
    for _ in range(3):
        hi = lax.reduce_precision(x, 8, 7)
        terms.append(hi.astype(BF))
        x = x - hi
    return terms


def split2(x):
    hi = x.astype(BF)
    return hi, (x - hi.astype(F32)).astype(BF)


def dot3(a, b, dims):
    (ah, al), (bh, bl) = a, b
    d = functools.partial(
        lax.dot_general, dimension_numbers=(dims, ((), ())), preferred_element_type=F32
    )
    return d(ah, bh) + (d(ah, bl) + d(al, bh))


def inverse_factor(block):
    tiles = BLOCK // 8
    row = lax.broadcasted_iota(jnp.int32, (8, BLOCK), 0)
    lane = lax.broadcasted_iota(jnp.int32, (8, BLOCK), 1)
    d = [block[8 * t : 8 * t + 8] for t in range(tiles)]
    m = [(lane == row + 8 * t).astype(F32) for t in range(tiles)]
    for j in range(BLOCK):
        t0, s = divmod(j, 8)
        drow = jnp.broadcast_to(d[t0][s : s + 1], (8, BLOCK))
        mrow = jnp.broadcast_to(m[t0][s : s + 1], (8, BLOCK))
        inv = 1.0 / jnp.broadcast_to(drow[:, j : j + 1], (8, BLOCK))
        dn = drow * inv
        mn = mrow * inv
        for t in range(t0, tiles):
            if t == t0 and s == 7:
                continue
            f = jnp.broadcast_to(d[t][:, j : j + 1], (8, BLOCK))
            if t == t0:
                f = jnp.where(row > s, f, 0.0)
            d[t] = d[t] - f * dn
            m[t] = m[t] - f * mn
    out = []
    for t in range(tiles):
        piv = jnp.sum(jnp.where(lane == row + 8 * t, d[t], 0.0), axis=1, keepdims=True)
        out.append(m[t] * lax.rsqrt(piv))
    return jnp.concatenate(out, axis=0)


def eliminate_kernel(x_ref, w_ref, u_hi, u_lo, work):
    n, width = x_ref.shape
    steps = n // BLOCK

    def step(k, carry):
        rows = pl.ds(pl.multiple_of(k * BLOCK, BLOCK), BLOCK)
        work[...] = x_ref[rows, :]
        for case in range(1, steps):

            @pl.when(k == case)
            def _():
                done = case * BLOCK
                left = (u_hi[:done, done : done + BLOCK], u_lo[:done, done : done + BLOCK])
                right = (u_hi[:done, done:], u_lo[:done, done:])
                work[:, done:] = work[:, done:] - dot3(left, right, ((0,), (0,)))

        inverse = split2(inverse_factor(work[:, rows]))
        solved = dot3(inverse, split2(work[...]), ((1,), (0,)))
        hi, lo = split2(solved)
        u_hi[rows, :] = hi
        u_lo[rows, :] = lo
        w_ref[rows, :] = solved[:, n:]
        return carry

    lax.fori_loop(0, steps, step, 0)


def eliminate(x):
    n, width = x.shape
    return pl.pallas_call(
        eliminate_kernel,
        out_shape=jax.ShapeDtypeStruct((n, width - n), F32),
        in_specs=[pl.BlockSpec(memory_space=pltpu.VMEM)],
        out_specs=pl.BlockSpec(memory_space=pltpu.VMEM),
        scratch_shapes=[
            pltpu.VMEM((n, width), BF),
            pltpu.VMEM((n, width), BF),
            pltpu.VMEM((BLOCK, width), F32),
        ],
        compiler_params=pltpu.CompilerParams(vmem_limit_bytes=56 * 1024 * 1024),
    )(x)


def on_device(occupations, table, weights, biases, heads, energies):
    row_count, orb = occupations.shape
    row_devices = lax.axis_size("row")
    col_devices = lax.axis_size("col")
    row_index = lax.axis_index("row")
    col_index = lax.axis_index("col")
    total = row_count * row_devices
    width = total // col_devices
    head_count = 2 * width
    hp = lax.Precision.HIGHEST

    occ = lax.all_gather(occupations.astype(BF), "row", axis=0, tiled=True)
    start = jnp.where(lax.iota(jnp.int32, row_devices) == row_index, energies[:, None], 0.0)
    rhs_all = lax.psum(start.T.reshape(-1), "row")

    level0 = table[:orb]
    steps = jnp.concatenate([table[orb : 2 * orb] - level0, table[2 * orb :] - level0], axis=0)
    base = jnp.sum(level0, axis=0)
    both = jnp.concatenate([steps, base[None]], axis=0)
    w = jnp.concatenate([weights[0], weights[1]], axis=1)
    folded = jnp.dot(both, w, precision=hp, preferred_element_type=F32)
    t_steps = jnp.concatenate(split3(folded[: 2 * orb])[:2], axis=0)
    t_base = folded[2 * orb]
    half_bias = 0.5 * biases.reshape(-1)
    gram = jnp.dot(both, both.T, precision=hp, preferred_element_type=F32)

    x = jnp.concatenate([(occ == 1).astype(BF), (occ == 2).astype(BF)], axis=1)
    x2 = jnp.concatenate([x, x], axis=1)
    g = gram[: 2 * orb, : 2 * orb]
    g_hi, g_lo, _ = split3(g)
    xg = jnp.dot(x, g_hi, preferred_element_type=F32) + jnp.dot(x, g_lo, preferred_element_type=F32)
    square = jnp.sum((xg + 2.0 * gram[2 * orb, : 2 * orb]) * x.astype(F32), axis=1)
    square = square + gram[2 * orb, 2 * orb]
    half_scale = 0.5 * lax.rsqrt(jnp.maximum(square, 0.0) / table.shape[1] + norm_eps)

    def gates(rows, scale, t, t0, b):
        return jnp.tanh(
            scale[:, None] * (jnp.dot(rows, t, preferred_element_type=F32) + t0) + b
        )

    mean = jnp.sum(gates(x2, half_scale, t_steps, t_base, half_bias), axis=0) / total
    consts = jnp.stack([t_base, half_bias, heads.reshape(-1) * (0.5 / math.sqrt(total)), mean])
    c1, c2, c3 = split3(consts)
    pack = jnp.concatenate([t_steps, c1, c2, c3, jnp.zeros_like(c1)], axis=0)
    pack = lax.all_gather(pack, "col", axis=1, tiled=True)
    t_all = pack[: 4 * orb]
    tail = pack[4 * orb :].astype(F32)
    t_base, half_bias, amp, mean = tail[0:4] + (tail[4:8] + tail[8:12])

    def pick(a, axis=0):
        return jnp.concatenate(
            [
                lax.slice_in_dim(a, 0, head_count, axis=axis),
                lax.dynamic_slice_in_dim(a, row_index * row_count, row_count, axis),
                lax.dynamic_slice_in_dim(a, col_index * width, width, axis),
            ],
            axis=axis,
        )

    centered = (
        amp * (gates(pick(x2), pick(half_scale), t_all, t_base, half_bias) - mean)
    ).astype(BF)
    ids = pick(lax.iota(jnp.int32, total))

    def gram_of(a, b, a_ids, b_ids):
        k = lax.dot_general(a, b, (((1,), (1,)), ((), ())), preferred_element_type=F32)
        return k + jnp.where(a_ids[:, None] == b_ids[None, :], diag_shift, 0.0)

    top = gram_of(centered[:head_count], centered, ids[:head_count], ids)
    mid = head_count + row_count
    own = gram_of(centered[head_count:mid], centered[mid:], ids[head_count:mid], ids[mid:])
    side = jnp.pad(rhs_all[:head_count, None], ((0, 0), (0, BLOCK - 1)))
    solved = eliminate(jnp.concatenate([top, side], axis=1))
    update = lax.dot_general(
        solved[:, :row_count],
        solved[:, row_count:],
        (((0,), (0,)), ((), ())),
        precision=lax.Precision.HIGH,
        preferred_element_type=F32,
    )
    schur = own - update[:, :width]
    front = solved[:, row_count + width]
    front = jnp.pad(front, (0, total - head_count))
    front = lax.dynamic_slice_in_dim(front, row_index * row_count, row_count)
    rest = energies - update[:, width]
    own_ids = ids[head_count:mid]
    return (schur, jnp.where(own_ids < head_count, front, rest))


def solution(mesh):
    placed = (P("row", None), P(), P(None, None, "col"), P(None, "col"), P(None, "col"), P("row"))
    return jax.shard_map(
        on_device,
        mesh=mesh,
        in_specs=placed,
        out_specs=(P("row", "col"), P("row")),
        check_vma=False,
    )
```

```python
import functools
import math

import jax
import jax.numpy as jnp
from jax import lax
from jax.experimental import pallas as pl
from jax.experimental.pallas import tpu as pltpu
from jax.sharding import PartitionSpec as P

norm_eps = 1e-06
diag_shift = 0.05
BLOCK = 128
BF = jnp.bfloat16
F32 = jnp.float32


def split3(x):
    terms = []
    for _ in range(3):
        hi = lax.reduce_precision(x, 8, 7)
        terms.append(hi.astype(BF))
        x = x - hi
    return terms


def split2(x):
    hi = x.astype(BF)
    return hi, (x - hi.astype(F32)).astype(BF)


def dot3(a, b, dims):
    (ah, al), (bh, bl) = a, b
    d = functools.partial(
        lax.dot_general, dimension_numbers=(dims, ((), ())), preferred_element_type=F32
    )
    return d(ah, bh) + (d(ah, bl) + d(al, bh))


def inverse_factor(block):
    tiles = BLOCK // 8
    row = lax.broadcasted_iota(jnp.int32, (8, BLOCK), 0)
    lane = lax.broadcasted_iota(jnp.int32, (8, BLOCK), 1)
    d = [block[8 * t : 8 * t + 8] for t in range(tiles)]
    m = [(lane == row + 8 * t).astype(F32) for t in range(tiles)]
    out = [jnp.zeros((8, BLOCK), F32) for _ in range(tiles)]

    def full(x):
        return jnp.broadcast_to(x, (8, BLOCK))

    for j in range(0, BLOCK, 4):
        t0, s = divmod(j, 8)
        d0, d1, d2, d3 = [full(d[t0][s + i : s + i + 1]) for i in range(4)]
        m0, m1, m2, m3 = [full(m[t0][s + i : s + i + 1]) for i in range(4)]
        a, b, e0, h0 = [full(d0[:, j + i : j + i + 1]) for i in range(4)]
        c, e1, h1 = [full(d1[:, j + i : j + i + 1]) for i in range(1, 4)]
        r, u = [full(d2[:, j + i : j + i + 1]) for i in range(2, 4)]
        v = full(d3[:, j + 3 : j + 4])

        inv = 1.0 / (a * c - b * b)
        ai, bi, ci = a * inv, b * inv, c * inv
        alpha2, beta2 = ci * e0 - bi * e1, ai * e1 - bi * e0
        alpha3, beta3 = ci * h0 - bi * h1, ai * h1 - bi * h0
        r = r - (e0 * alpha2 + e1 * beta2)
        u = u - (e0 * alpha3 + e1 * beta3)
        v = v - (h0 * alpha3 + h1 * beta3)
        inv2 = 1.0 / (r * v - u * u)
        ri, ui, vi = r * inv2, u * inv2, v * inv2

        q0, q1 = ci * d0 - bi * d1, ai * d1 - bi * d0
        p0, p1 = ci * m0 - bi * m1, ai * m1 - bi * m0
        d2, d3 = d2 - (e0 * q0 + e1 * q1), d3 - (h0 * q0 + h1 * q1)
        m2, m3 = m2 - (e0 * p0 + e1 * p1), m3 - (h0 * p0 + h1 * p1)
        q2, q3 = vi * d2 - ui * d3, ri * d3 - ui * d2
        p2, p3 = vi * m2 - ui * m3, ri * m3 - ui * m2

        ba, ur = b / a, u / r
        done = (
            m0 * lax.rsqrt(a),
            (m1 - ba * m0) * lax.rsqrt(c - ba * b),
            m2 * lax.rsqrt(r),
            (m3 - ur * m2) * lax.rsqrt(v - ur * u),
        )
        for i in range(4):
            out[t0] = jnp.where(row == s + i, done[i], out[t0])

        for t in range(t0, tiles):
            if t == t0 and s == 4:
                continue
            f0, f1, f2, f3 = [full(d[t][:, j + i : j + i + 1]) for i in range(4)]
            f2 = f2 - (f0 * alpha2 + f1 * beta2)
            f3 = f3 - (f0 * alpha3 + f1 * beta3)
            if t == t0:
                f0, f1, f2, f3 = [jnp.where(row > 3, f, 0.0) for f in (f0, f1, f2, f3)]
            d[t] = d[t] - ((f0 * q0 + f1 * q1) + (f2 * q2 + f3 * q3))
            m[t] = m[t] - ((f0 * p0 + f1 * p1) + (f2 * p2 + f3 * p3))
    return jnp.concatenate(out, axis=0)


def eliminate_kernel(x_ref, update_ref, side_ref, u_hi, u_lo, work):
    n, width = x_ref.shape
    row_count = update_ref.shape[0]
    steps = n // BLOCK

    def step(k, carry):
        rows = pl.ds(pl.multiple_of(k * BLOCK, BLOCK), BLOCK)
        work[...] = x_ref[rows, :]
        for case in range(1, steps):

            @pl.when(k == case)
            def _():
                done = case * BLOCK
                left = (u_hi[:done, done : done + BLOCK], u_lo[:done, done : done + BLOCK])
                right = (u_hi[:done, done:], u_lo[:done, done:])
                work[:, done:] = work[:, done:] - dot3(left, right, ((0,), (0,)))

        inverse = split2(inverse_factor(work[:, rows]))
        solved = dot3(inverse, split2(work[...]), ((1,), (0,)))
        hi, lo = split2(solved)
        u_hi[rows, :] = hi
        u_lo[rows, :] = lo
        side_ref[rows, :] = solved[:, width - BLOCK :]
        return carry

    lax.fori_loop(0, steps, step, 0)

    def product(i, carry):
        cols = pl.ds(pl.multiple_of(n + i * BLOCK, BLOCK), BLOCK)
        rows = pl.ds(pl.multiple_of(i * BLOCK, BLOCK), BLOCK)
        left = (u_hi[:, cols], u_lo[:, cols])
        right = (u_hi[:, n + row_count :], u_lo[:, n + row_count :])
        update_ref[rows, :] = dot3(left, right, ((0,), (0,)))
        return carry

    lax.fori_loop(0, row_count // BLOCK, product, 0)


def eliminate(x, row_count):
    n, width = x.shape
    return pl.pallas_call(
        eliminate_kernel,
        out_shape=(
            jax.ShapeDtypeStruct((row_count, width - n - row_count), F32),
            jax.ShapeDtypeStruct((n, BLOCK), F32),
        ),
        in_specs=[pl.BlockSpec(memory_space=pltpu.VMEM)],
        out_specs=(
            pl.BlockSpec(memory_space=pltpu.VMEM),
            pl.BlockSpec(memory_space=pltpu.VMEM),
        ),
        scratch_shapes=[
            pltpu.VMEM((n, width), BF),
            pltpu.VMEM((n, width), BF),
            pltpu.VMEM((BLOCK, width), F32),
        ],
        compiler_params=pltpu.CompilerParams(vmem_limit_bytes=56 * 1024 * 1024),
    )(x)


def on_device(occupations, table, weights, biases, heads, energies):
    row_count, orb = occupations.shape
    row_devices = lax.axis_size("row")
    col_devices = lax.axis_size("col")
    row_index = lax.axis_index("row")
    col_index = lax.axis_index("col")
    total = row_count * row_devices
    width = total // col_devices
    head_count = 2 * width
    hp = lax.Precision.HIGHEST

    terms = jnp.concatenate([e.reshape(-1, orb) for e in split3(energies)], axis=0)
    sent = jnp.concatenate([occupations.astype(BF), terms], axis=0)
    came = lax.all_gather(sent, "row", axis=0)
    occ = came[:, :row_count].reshape(total, orb)
    terms = came[:, row_count:].astype(F32).reshape(row_devices, 3, row_count)
    rhs_all = (terms[:, 0] + (terms[:, 1] + terms[:, 2])).reshape(total)

    level0 = table[:orb]
    steps = jnp.concatenate([table[orb : 2 * orb] - level0, table[2 * orb :] - level0], axis=0)
    base = jnp.sum(level0, axis=0)
    both = jnp.concatenate([steps, base[None]], axis=0)
    w = jnp.concatenate([weights[0], weights[1]], axis=1)
    folded = jnp.dot(both, w, precision=hp, preferred_element_type=F32)
    t_steps = jnp.concatenate(split3(folded[: 2 * orb])[:2], axis=0)
    t_base = folded[2 * orb]
    half_bias = 0.5 * biases.reshape(-1)
    gram = jnp.dot(both, both.T, precision=hp, preferred_element_type=F32)

    x = jnp.concatenate([(occ == 1).astype(BF), (occ == 2).astype(BF)], axis=1)
    x2 = jnp.concatenate([x, x], axis=1)
    g = gram[: 2 * orb, : 2 * orb]
    g_hi, g_lo, _ = split3(g)
    xg = jnp.dot(x, g_hi, preferred_element_type=F32) + jnp.dot(x, g_lo, preferred_element_type=F32)
    square = jnp.sum((xg + 2.0 * gram[2 * orb, : 2 * orb]) * x.astype(F32), axis=1)
    square = square + gram[2 * orb, 2 * orb]
    half_scale = 0.5 * lax.rsqrt(jnp.maximum(square, 0.0) / table.shape[1] + norm_eps)

    def gates(rows, scale, t, t0, b):
        return jnp.tanh(
            scale[:, None] * (jnp.dot(rows, t, preferred_element_type=F32) + t0) + b
        )

    mean = jnp.sum(gates(x2, half_scale, t_steps, t_base, half_bias), axis=0) / total
    consts = jnp.stack([t_base, half_bias, heads.reshape(-1) * (0.5 / math.sqrt(total)), mean])
    c1, c2, c3 = split3(consts)
    pack = jnp.concatenate([t_steps, c1, c2, c3, jnp.zeros_like(c1)], axis=0)
    pack = lax.all_gather(pack, "col", axis=1, tiled=True)
    t_all = pack[: 4 * orb]
    tail = pack[4 * orb :].astype(F32)
    t_base, half_bias, amp, mean = tail[0:4] + (tail[4:8] + tail[8:12])

    def pick(a, axis=0):
        return jnp.concatenate(
            [
                lax.slice_in_dim(a, 0, head_count, axis=axis),
                lax.dynamic_slice_in_dim(a, row_index * row_count, row_count, axis),
                lax.dynamic_slice_in_dim(a, col_index * width, width, axis),
            ],
            axis=axis,
        )

    centered = (
        amp * (gates(pick(x2), pick(half_scale), t_all, t_base, half_bias) - mean)
    ).astype(BF)
    ids = pick(lax.iota(jnp.int32, total))

    def gram_of(a, b, a_ids, b_ids):
        k = lax.dot_general(a, b, (((1,), (1,)), ((), ())), preferred_element_type=F32)
        return k + jnp.where(a_ids[:, None] == b_ids[None, :], diag_shift, 0.0)

    top = gram_of(centered[:head_count], centered, ids[:head_count], ids)
    mid = head_count + row_count
    own = gram_of(centered[head_count:mid], centered[mid:], ids[head_count:mid], ids[mid:])
    side = jnp.pad(rhs_all[:head_count, None], ((0, 0), (0, BLOCK - 1)))
    update, side = eliminate(jnp.concatenate([top, side], axis=1), row_count)
    schur = own - update[:, :width]
    front = side[:, 0]
    front = jnp.pad(front, (0, total - head_count))
    front = lax.dynamic_slice_in_dim(front, row_index * row_count, row_count)
    rest = energies - update[:, width]
    own_ids = ids[head_count:mid]
    return (schur, jnp.where(own_ids < head_count, front, rest))


def solution(mesh):
    placed = (P("row", None), P(), P(None, None, "col"), P(None, "col"), P(None, "col"), P("row"))
    return jax.shard_map(
        on_device,
        mesh=mesh,
        in_specs=placed,
        out_specs=(P("row", "col"), P("row")),
        check_vma=False,
    )
```
